32 devices in a mesh: sec: 4 (over y, x), ta: 8 (over z, core).
Axes of the slice: x: 2, y: 2, z: 4, core: 2. Of those that a mesh axis runs over, the one named last changes fastest.
Arguments:
- sink_vectors: bfloat16 [2, 8, 4096, 512], P(None, 'ta', 'sec'), may hold values from -0.0625 to 0.0625
- propagators: bfloat16 [3, 2, 8, 4096, 512], P(None, None, 'ta', 'sec'), may hold values from -6 to 6
- live_rows: int32 [4], replicated, may hold values from 512 to 1024, as said below
- source_times: int32 [3], replicated, may hold values from 0 to 7
Outputs:
- sandwich: bfloat16 [3, 3, 3, 2, 8, 512, 512], P(None, None, None, None, 'ta', 'sec')
The draws below stay inside these ranges and needn't reach their ends.
Inputs may be any that keep to these rules, and one draw needn't show every extreme that they name: `live_rows`: some section has exactly 1024 live rows in every draw.
All inputs are finite; a program needn't handle non-finite values.
Results may differ from the reference program's by a relative error of at most 0.02.
Values may be sent and summed in bfloat16 or wider, within the bound.
No kernel may reach another device: no remote copies, remote signals or barrier semaphores. Data moves between devices by JAX's collectives and lax.ppermute only.
A program may use at most 64 MiB of HBM per device.

```python
import jax
import jax.numpy as jnp
from jax import lax

ORDER = 512
SOURCES = 3
STOPS = 3
ROWS_DEV = 1024
SITES = 4096
TIMES = 8
N_SEC = 4


def draw_live_rows(key, part):
    counts = jax.random.randint(key, (N_SEC,), ROWS_DEV // 2, ROWS_DEV + 1)
    chosen = jax.random.randint(jax.random.fold_in(key, 7), (), 0, N_SEC)
    return counts.at[chosen].set(ROWS_DEV).astype(jnp.int32)


def levels(stream_key, dims, pieces, least, high):
    loudness = 1.0
    for dim, parts in pieces:
        heights = jax.random.uniform(jax.random.fold_in(jax.random.fold_in(stream_key, 6), dim), (parts,), jnp.float32, least / len(pieces), high / len(pieces))
        loudness = loudness * jnp.repeat(jnp.exp(heights), dims[dim] // parts).reshape((-1,) + (1,) * (len(dims) - 1 - dim))
    return loudness


def noise(own_key, extent, width, limit, cuts=(), kind=jnp.bfloat16):
    level = levels(own_key, extent, cuts, -0.22, 0.18) if cuts else 1.0
    values = jax.random.normal(own_key, extent, jnp.float32) * width * level
    return jnp.minimum(jnp.maximum(values, -limit), limit).astype(kind)


def setup_inputs(seed: int = 0) -> dict:
    key_of = jax.random.split(jax.random.key(seed), 5)
    return {
        "sink_vectors": noise(key_of[0], (2, TIMES, SITES, ORDER), (2 * SITES) ** -0.5, 0.0625, ((1, 8), (2, 4))),
        "propagators": noise(key_of[1], (SOURCES, 2, TIMES, SITES, ORDER), 1.0, 6.0, ((2, 8), (3, 4))),
        "live_rows": draw_live_rows(jax.random.fold_in(key_of[4], 71), 0),
        "source_times": jax.random.randint(key_of[3], (SOURCES,), 0, TIMES).astype(jnp.int32),
    }


def reference(sink_vectors, propagators, live_rows, source_times):
    live_mask = (jnp.arange(ROWS_DEV, dtype=jnp.int32)[None, :] < live_rows[:, None]).astype(jnp.bfloat16).reshape(-1)

    def meson_at(moment):
        sink_rows = lax.dynamic_index_in_dim(sink_vectors, moment, 1, keepdims=False) * live_mask[None, :, None]
        prop_rows = lax.dynamic_index_in_dim(propagators, moment, 2, keepdims=False)
        sink_split = sink_rows.reshape(2, N_SEC, ROWS_DEV, ORDER).astype(jnp.float32)
        prop_split = prop_rows.reshape(SOURCES, 2, N_SEC, ROWS_DEV, ORDER).astype(jnp.float32)
        products = jnp.einsum("cnrx,sdnry->nxscdy", sink_split, prop_split)
        real_part = products[:, :, :, 0, 0] + products[:, :, :, 1, 1]
        imag_part = products[:, :, :, 0, 1] - products[:, :, :, 1, 0]
        stacked = jnp.stack((real_part, imag_part), 3)
        sign_flip = jnp.where(moment < source_times, -1.0, 1.0).astype(jnp.float32)
        partial_low = (stacked * sign_flip[None, None, :, None, None]).astype(jnp.bfloat16)
        partial_low = lax.optimization_barrier(partial_low)
        return jnp.sum(partial_low.astype(jnp.float32), 0).astype(jnp.bfloat16)

    mesons = lax.map(meson_at, jnp.arange(TIMES, dtype=jnp.int32))
    scale_factor = 0.5 * ORDER ** -0.5

    def sandwich_at(pair):
        local_full, remote_full = pair
        products = jnp.einsum("iacx,xbdj->abcdij", local_full.astype(jnp.float32), remote_full.astype(jnp.float32))
        real_part = products[:, :, 0, 0] - products[:, :, 1, 1]
        imag_part = products[:, :, 0, 1] + products[:, :, 1, 0]
        return (jnp.stack((real_part, imag_part), 2) * scale_factor).astype(jnp.bfloat16)

    results = []
    for stop_index in range(STOPS):
        remote = jnp.roll(mesons, stop_index + 1, axis=0)
        results.append(lax.map(sandwich_at, (mesons, remote)))
    stacked_all = jnp.stack(results, 0)
    return jnp.transpose(stacked_all, (0, 2, 3, 4, 1, 5, 6))
```

```python
import functools

import jax
import jax.numpy as jnp
from jax import lax
from jax.experimental import pallas as pl
from jax.experimental.pallas import tpu as pltpu
from jax.sharding import PartitionSpec as P

STOPS = 3


def shifted(value, axis, steps):
    count = lax.axis_size(axis)
    pairs = [(source, (source + steps) % count) for source in range(count)]
    return lax.ppermute(value, axis, pairs)


def exchanged(value, axis, bit):
    count = lax.axis_size(axis)
    return lax.ppermute(value, axis, [(source, source ^ bit) for source in range(count)])


def reversed_bits(value, width):
    return sum(((value >> place) & 1) << (width - 1 - place) for place in range(width))


def product_kernel(sections, source, scalars, *refs):
    sinks, prop = refs[:sections], refs[sections]
    keep_real, send_real, keep_imag, send_imag = refs[sections + 1 :]
    half = sections // 2
    width = sections.bit_length() - 1
    sign = jnp.where(scalars[1 + source] == 1, -1.0, 1.0).astype(jnp.float32)
    prop_real, prop_imag = prop[0, 0, 0], prop[0, 1, 0]
    for q in range(sections):
        block = sinks[q]
        rows = block.shape[2]
        sink = block[...].reshape(2 * rows, block.shape[3])
        with_real = jnp.dot(sink, prop_real, preferred_element_type=jnp.float32)
        with_imag = jnp.dot(sink, prop_imag, preferred_element_type=jnp.float32)
        real = (with_real[:rows] + with_imag[rows:]) * sign
        imag = (with_imag[:rows] - with_real[rows:]) * sign
        slot = reversed_bits(q, width)
        target = keep_real if slot < half else send_real
        target[slot % half] = real.astype(jnp.bfloat16)
        target = keep_imag if q < half else send_imag
        target[q % half] = imag.astype(jnp.bfloat16)


def products(scalars, sink_columns, propagators, source, sections):
    _, order, depth = sink_columns.shape
    rows = order // sections
    width = 256
    sinks = sink_columns.reshape(2, sections, rows, depth)
    columns = propagators.shape[4]
    half = jax.ShapeDtypeStruct((sections // 2, rows, columns), jnp.bfloat16)
    return pl.pallas_call(
        functools.partial(product_kernel, sections, source),
        grid_spec=pltpu.PrefetchScalarGridSpec(
            num_scalar_prefetch=1,
            grid=(columns // width,),
            in_specs=[
                pl.BlockSpec((2, 1, rows, depth), lambda j, s, q=q: (0, s[0] ^ q, 0, 0))
                for q in range(sections)
            ]
            + [pl.BlockSpec((1, 2, 1, depth, width), lambda j, s: (source, 0, 0, 0, j))],
            out_specs=[pl.BlockSpec((sections // 2, rows, width), lambda j, s: (0, 0, j))] * 4,
        ),
        out_shape=[half] * 4,
        cost_estimate=pl.CostEstimate(
            flops=8 * order * depth * columns,
            bytes_accessed=4 * depth * (order + columns) + 4 * order * columns,
            transcendentals=0,
        ),
        name="products",
    )(scalars, *([sinks] * sections), propagators)


def reduced(keep_real, send_real, keep_imag, send_imag, width):
    for step in range(width):
        got_real = exchanged(send_real, "sec", 1 << step)
        got_imag = exchanged(send_imag, "sec", 1 << (width - 1 - step))
        real = keep_real.astype(jnp.float32) + got_real.astype(jnp.float32)
        imag = keep_imag.astype(jnp.float32) + got_imag.astype(jnp.float32)
        real, imag = real.astype(jnp.bfloat16), imag.astype(jnp.bfloat16)
        half = real.shape[0] // 2
        if half:
            keep_real, send_real = real[:half], real[half:]
            keep_imag, send_imag = imag[:half], imag[half:]
    return jnp.concatenate((real, imag), 0)


def gathered(own, width):
    pieces = [own]
    for q in range(1, 1 << width):
        high = 1 << (q.bit_length() - 1)
        low = q & -q
        if high == low:
            pieces.append(exchanged(own, "sec", high))
        else:
            first, second = pieces[q ^ high], pieces[q ^ low]
            pieces.append((exchanged(first[0], "sec", high), exchanged(second[1], "sec", low)))
    return pieces


def sandwich_kernel(scale, paired, names, scalars, *refs):
    left_real, left_imag = refs[0], refs[1]
    blocks = list(refs[2 : 2 + names])
    out = refs[-1]
    real, imag = [], []
    for pair in paired:
        if pair:
            real.append(blocks.pop(0)[...])
            imag.append(blocks.pop(0)[...])
        else:
            block = blocks.pop(0)
            real.append(block[0])
            imag.append(block[1])
    right_real, right_imag = jnp.concatenate(real, 0), jnp.concatenate(imag, 0)
    dot = functools.partial(jnp.dot, preferred_element_type=jnp.float32)
    one, two = left_real[...], left_imag[...]
    shape = (out.shape[1],) + out.shape[5:]
    out[0, :, 0, 0, 0] = (
        ((dot(one, right_real) - dot(two, right_imag)) * scale).astype(jnp.bfloat16).reshape(shape)
    )
    out[0, :, 0, 1, 0] = (
        ((dot(one, right_imag) + dot(two, right_real)) * scale).astype(jnp.bfloat16).reshape(shape)
    )


def sandwich(buffer, stop, source, left_real, left_imag, pieces, shape):
    paired = tuple(isinstance(piece, tuple) for piece in pieces)
    blocks = [part for piece in pieces for part in (piece if isinstance(piece, tuple) else (piece,))]
    order = left_real.shape[1]
    operands = [left_real, left_imag, *blocks]

    def whole(value):
        return pl.BlockSpec(value.shape, lambda i, s, rank=value.ndim: (0,) * rank)

    in_specs = [whole(value) for value in operands]
    aliases = {}
    if buffer is not None:
        aliases = {1 + len(operands): 0}
        in_specs.append(pl.BlockSpec(memory_space=pl.ANY))
        operands.append(buffer)
    block = (1, shape[1], 1, 2, 1) + tuple(shape[5:])
    return pl.pallas_call(
        functools.partial(sandwich_kernel, 0.5 * order ** (-0.5), paired, len(blocks)),
        grid_spec=pltpu.PrefetchScalarGridSpec(
            num_scalar_prefetch=1,
            grid=(1,),
            in_specs=in_specs,
            out_specs=pl.BlockSpec(block, lambda i, s: (s[0], 0, source, 0, 0, 0, 0)),
        ),
        out_shape=jax.ShapeDtypeStruct(shape, jnp.bfloat16),
        input_output_aliases=aliases,
        cost_estimate=pl.CostEstimate(
            flops=8 * left_real.shape[0] * order * shape[6],
            bytes_accessed=4 * order * shape[6] + 8 * left_real.size,
            transcendentals=0,
        ),
        name="sandwich",
    )(jnp.reshape(stop, (1,)).astype(jnp.int32), *operands)


def local(sink_vectors, propagators, live_rows, source_times):
    sections = lax.axis_size("sec")
    width = sections.bit_length() - 1
    section = lax.axis_index("sec")
    moment = lax.axis_index("ta")
    first_core = moment % 2 == 0
    sources = propagators.shape[0]
    sink_rows = sink_vectors[:, 0]
    depth, order = sink_rows.shape[1:]
    rows = order // sections
    live = lax.broadcasted_iota(jnp.int32, (1, depth, 1), 1) < live_rows[section]
    sink_columns = jnp.swapaxes(jnp.where(live, sink_rows, jnp.zeros_like(sink_rows)), 1, 2)
    scalars = jnp.concatenate(
        (jnp.reshape(section, (1,)), (moment < source_times).astype(jnp.int32))
    ).astype(jnp.int32)

    own = []
    for source in range(sources):
        halves = products(scalars, sink_columns, propagators, source, sections)
        own.append(reduced(*halves, width))
    second = [shifted(value, "ta", 2) for value in own]
    other = [
        shifted(jnp.where(first_core, own[s], second[s]), "ta", 1) for s in range(sources)
    ]

    left = jnp.stack(own, 1)
    left = jnp.concatenate(
        [
            lax.dynamic_slice_in_dim(left, (section ^ q) * rows, rows, axis=3)
            for q in range(sections)
        ],
        3,
    ).reshape(2, sources * rows, order)
    left_real, left_imag = left[0], left[1]

    shape = (STOPS, sources, sources, 2, 1, rows, order)
    near_stop = jnp.where(first_core, 0, 2)
    result = None
    for s in range(sources):
        pieces = gathered(second[s], width)
        swapped = jax.tree.map(lambda value: exchanged(value, "ta", 1), pieces)
        result = sandwich(result, jnp.int32(1), s, left_real, left_imag, pieces, shape)
        result = sandwich(result, near_stop, s, left_real, left_imag, swapped, shape)
    for s in range(sources):
        pieces = gathered(other[s], width)
        result = sandwich(result, 2 - near_stop, s, left_real, left_imag, pieces, shape)
    return result


def solution(mesh):
    return jax.shard_map(
        local,
        mesh=mesh,
        in_specs=(P(None, "ta", "sec", None), P(None, None, "ta", "sec", None), P(), P()),
        out_specs=P(None, None, None, None, "ta", "sec", None),
        check_vma=False,
    )
```

```python
import functools

import jax
import jax.numpy as jnp
from jax import lax
from jax.experimental import pallas as pl
from jax.experimental.pallas import tpu as pltpu
from jax.sharding import PartitionSpec as P

STOPS = 3
dot = functools.partial(jnp.dot, preferred_element_type=jnp.float32)


def shifted(value, steps):
    count = lax.axis_size("ta")
    pairs = [(source, (source + steps) % count) for source in range(count)]
    return lax.ppermute(value, "ta", pairs)


def exchanged(value, axis, bit):
    count = lax.axis_size(axis)
    return lax.ppermute(value, axis, [(source, source ^ bit) for source in range(count)])


def reversed_bits(value, width):
    return sum(((value >> place) & 1) << (width - 1 - place) for place in range(width))


def over_rows(left, right):
    return lax.dot_general(
        left, right, (((0,), (0,)), ((), ())), preferred_element_type=jnp.float32
    )


def product_kernel(
    sections, source, live_rows, source_times, sink_hbm, prop_hbm,
    keep_real, send_real, keep_imag, send_imag, sink, prop, real, imag, sems,
):
    section = lax.axis_index("sec")
    copies = []
    for part in range(2):
        copies.append(pltpu.make_async_copy(sink_hbm.at[part, 0], sink.at[part], sems.at[part, 0]))
        copies.append(
            pltpu.make_async_copy(prop_hbm.at[source, part, 0], prop.at[part], sems.at[part, 1])
        )
    for copy in copies:
        copy.start()
    depth, order = sink.shape[1:]
    live = lax.broadcasted_iota(jnp.int32, (depth, order), 0) < live_rows[section]
    sign = jnp.where(lax.axis_index("ta") < source_times[source], -1.0, 1.0).astype(jnp.float32)
    none = jnp.zeros((depth, order), jnp.bfloat16)
    copies[0].wait()
    sink_real = jnp.where(live, sink[0], none)
    copies[1].wait()
    first = over_rows(sink_real, prop[0])
    copies[2].wait()
    sink_imag = jnp.where(live, sink[1], none)
    copies[3].wait()
    real[...] = ((first + over_rows(sink_imag, prop[1])) * sign).astype(jnp.bfloat16)
    imag[...] = (
        (over_rows(sink_real, prop[1]) - over_rows(sink_imag, prop[0])) * sign
    ).astype(jnp.bfloat16)
    half = sections // 2
    width = sections.bit_length() - 1
    rows = order // sections
    for q in range(sections):
        window = pl.ds(pl.multiple_of((section ^ q) * rows, rows), rows)
        slot = reversed_bits(q, width)
        (keep_real if slot < half else send_real)[slot % half] = real[window, :]
        (keep_imag if q < half else send_imag)[q % half] = imag[window, :]


def products(live_rows, source_times, sink_vectors, propagators, source, sections):
    _, _, depth, order = sink_vectors.shape
    columns = propagators.shape[4]
    half = jax.ShapeDtypeStruct((sections // 2, order // sections, columns), jnp.bfloat16)
    scalar = pl.BlockSpec(memory_space=pltpu.SMEM)
    return pl.pallas_call(
        functools.partial(product_kernel, sections, source),
        in_specs=[scalar, scalar]
        + [pl.BlockSpec(memory_space=pltpu.HBM)] * 2,
        out_specs=[pl.BlockSpec(memory_space=pltpu.VMEM)] * 4,
        out_shape=[half] * 4,
        scratch_shapes=[
            pltpu.VMEM((2, depth, order), jnp.bfloat16),
            pltpu.VMEM((2, depth, columns), jnp.bfloat16),
            pltpu.VMEM((order, columns), jnp.bfloat16),
            pltpu.VMEM((order, columns), jnp.bfloat16),
            pltpu.SemaphoreType.DMA((2, 2)),
        ],
        compiler_params=pltpu.CompilerParams(vmem_limit_bytes=20 << 20),
        cost_estimate=pl.CostEstimate(
            flops=8 * order * depth * columns,
            bytes_accessed=4 * depth * (order + columns) + 4 * order * columns,
            transcendentals=0,
        ),
    )(live_rows, source_times, sink_vectors, propagators)


def reduced(keep_real, send_real, keep_imag, send_imag, width):
    for step in range(width):
        got_real = exchanged(send_real, "sec", 1 << step)
        got_imag = exchanged(send_imag, "sec", 1 << (width - 1 - step))
        real = keep_real.astype(jnp.float32) + got_real.astype(jnp.float32)
        imag = keep_imag.astype(jnp.float32) + got_imag.astype(jnp.float32)
        real, imag = real.astype(jnp.bfloat16), imag.astype(jnp.bfloat16)
        half = real.shape[0] // 2
        if half:
            keep_real, send_real = real[:half], real[half:]
            keep_imag, send_imag = imag[:half], imag[half:]
    return jnp.concatenate((real, imag), 0)


def gathered(own, width):
    pieces = [own]
    for q in range(1, 1 << width):
        high = 1 << (q.bit_length() - 1)
        low = q & -q
        if high == low:
            pieces.append(exchanged(own, "sec", high))
        else:
            first, second = pieces[q ^ high], pieces[q ^ low]
            pieces.append((exchanged(first[0], "sec", high), exchanged(second[1], "sec", low)))
    return pieces


def sandwich_kernel(scale, paired, names, source, kind, aliased, *refs):
    left_real, left_imag = refs[0], refs[1]
    blocks = list(refs[2 : 2 + names])
    out, tile, sems = refs[2 + names + aliased :]
    real, imag = [], []
    for pair in paired:
        if pair:
            real.append(blocks.pop(0)[...])
            imag.append(blocks.pop(0)[...])
        else:
            block = blocks.pop(0)
            real.append(block[0])
            imag.append(block[1])
    right_real, right_imag = jnp.concatenate(real, 0), jnp.concatenate(imag, 0)
    one, two = left_real[...], left_imag[...]
    parity = lax.axis_index("ta") % 2
    stop = (2 * parity, 1, 2 - 2 * parity)[kind]
    shape = tile.shape[1:]
    copies = []
    for part in range(2):
        if part == 0:
            value = dot(one, right_real) - dot(two, right_imag)
        else:
            value = dot(one, right_imag) + dot(two, right_real)
        tile[part] = (value * scale).astype(jnp.bfloat16).reshape(shape)
        copies.append(
            pltpu.make_async_copy(tile.at[part], out.at[stop, :, source, part, 0], sems.at[part])
        )
        copies[-1].start()
    for copy in copies:
        copy.wait()


def sandwich(buffer, kind, source, left_real, left_imag, pieces, shape):
    paired = tuple(isinstance(piece, tuple) for piece in pieces)
    blocks = [part for piece in pieces for part in (piece if isinstance(piece, tuple) else (piece,))]
    order = left_real.shape[1]
    operands = [left_real, left_imag, *blocks]
    in_specs = [pl.BlockSpec(memory_space=pltpu.VMEM)] * len(operands)
    aliases = {}
    if buffer is not None:
        aliases = {len(operands): 0}
        in_specs.append(pl.BlockSpec(memory_space=pltpu.HBM))
        operands.append(buffer)
    return pl.pallas_call(
        functools.partial(
            sandwich_kernel, 0.5 * order ** (-0.5), paired, len(blocks), source, kind,
            len(aliases),
        ),
        in_specs=in_specs,
        out_specs=pl.BlockSpec(memory_space=pltpu.HBM),
        out_shape=jax.ShapeDtypeStruct(shape, jnp.bfloat16),
        scratch_shapes=[
            pltpu.VMEM((2, shape[1]) + tuple(shape[5:]), jnp.bfloat16),
            pltpu.SemaphoreType.DMA((2,)),
        ],
        input_output_aliases=aliases,
        compiler_params=pltpu.CompilerParams(vmem_limit_bytes=12 << 20),
        cost_estimate=pl.CostEstimate(
            flops=8 * left_real.shape[0] * order * shape[6],
            bytes_accessed=4 * order * shape[6] + 8 * left_real.size,
            transcendentals=0,
        ),
    )(*operands)


def body(sink_vectors, propagators, live_rows, source_times):
    sections = lax.axis_size("sec")
    width = sections.bit_length() - 1
    section = lax.axis_index("sec")
    first_core = lax.axis_index("ta") % 2 == 0
    sources = propagators.shape[0]
    order = sink_vectors.shape[3]
    rows = order // sections

    own = []
    for s in range(sources):
        halves = products(live_rows, source_times, sink_vectors, propagators, s, sections)
        own.append(reduced(*halves, width))
    second = [shifted(own[s], 2) for s in range(sources)]
    other = [shifted(jnp.where(first_core, own[s], second[s]), 1) for s in range(sources)]

    left = jnp.stack(own, 1)
    left = jnp.concatenate(
        [
            lax.dynamic_slice_in_dim(left, (section ^ q) * rows, rows, axis=3)
            for q in range(sections)
        ],
        3,
    ).reshape(2, sources * rows, order)
    left_real, left_imag = left[0], left[1]

    shape = (STOPS, sources, sources, 2, 1, rows, order)
    result = None
    for s in range(sources):
        pieces = gathered(second[s], width)
        leaves, tree = jax.tree.flatten(pieces)
        swapped = tree.unflatten([exchanged(leaf, "ta", 1) for leaf in leaves])
        result = sandwich(result, 1, s, left_real, left_imag, pieces, shape)
        result = sandwich(result, 0, s, left_real, left_imag, swapped, shape)
    for s in range(sources):
        pieces = gathered(other[s], width)
        result = sandwich(result, 2, s, left_real, left_imag, pieces, shape)
    return result


def solution(mesh):
    return jax.shard_map(
        body,
        mesh=mesh,
        in_specs=(P(None, "ta", "sec", None), P(None, None, "ta", "sec", None), P(), P()),
        out_specs=P(None, None, None, None, "ta", "sec", None),
        check_vma=False,
    )
```

```python
import functools

import jax
import jax.numpy as jnp
from jax import lax
from jax.experimental import pallas as pl
from jax.experimental.pallas import tpu as pltpu
from jax.sharding import PartitionSpec as P

STOPS = 3
dot = functools.partial(jnp.dot, preferred_element_type=jnp.float32)


def shifted(value, steps):
    count = lax.axis_size("ta")
    pairs = [(source, (source + steps) % count) for source in range(count)]
    return lax.ppermute(value, "ta", pairs)


def exchanged(value, axis, bit):
    count = lax.axis_size(axis)
    return lax.ppermute(value, axis, [(source, source ^ bit) for source in range(count)])


def reversed_bits(value, width):
    return sum(((value >> place) & 1) << (width - 1 - place) for place in range(width))


def over_rows(left, right):
    return lax.dot_general(
        left, right, (((0,), (0,)), ((), ())), preferred_element_type=jnp.float32
    )


def product_kernel(sections, source, sources, *refs):
    refs = list(refs)
    first, last = source == 0, source == sources - 1
    if first:
        live_hbm, times_hbm, sink_hbm, prop_hbm = refs[:4]
        refs = refs[4:]
    else:
        times_hbm, sink, prop, prop_hbm = refs[:4]
        refs = refs[4:]
    keep_real, send_real, keep_imag, send_imag = refs[:4]
    refs = refs[4:]
    if first:
        sink = refs.pop(0)
    following = None if last else refs.pop(0)
    real, imag, times, sems, index_sems = refs[:5]
    refs = refs[5:]
    index_copies = [pltpu.make_async_copy(times_hbm, times, index_sems.at[0])]
    copies = []
    if first:
        live_rows, raw, prop = refs
        index_copies.append(pltpu.make_async_copy(live_hbm, live_rows, index_sems.at[1]))
        for part in range(2):
            copies.append(pltpu.make_async_copy(sink_hbm.at[part, 0], raw.at[part], sems.at[part]))
            copies.append(
                pltpu.make_async_copy(prop_hbm.at[0, part, 0], prop.at[part], sems.at[2 + part])
            )
    if not last:
        for part in range(2):
            copies.append(
                pltpu.make_async_copy(
                    prop_hbm.at[source + 1, part, 0], following.at[part], sems.at[4 + part]
                )
            )
    for copy in index_copies + copies:
        copy.start()
    section = lax.axis_index("sec")
    depth, order = sink.shape[1:]
    for copy in index_copies:
        copy.wait()
    sign = jnp.where(lax.axis_index("ta") < times[source], -1.0, 1.0).astype(jnp.float32)
    if first:
        live = lax.broadcasted_iota(jnp.int32, (depth, order), 0) < live_rows[section]
        for part in range(2):
            copies.pop(0).wait()
            sink[part] = jnp.where(live, raw[part], jnp.zeros((depth, order), jnp.bfloat16))
            copies.pop(0).wait()
            if part == 0:
                start = over_rows(sink[0], prop[0])
        real[...] = ((start + over_rows(sink[1], prop[1])) * sign).astype(jnp.bfloat16)
    else:
        real[...] = (
            (over_rows(sink[0], prop[0]) + over_rows(sink[1], prop[1])) * sign
        ).astype(jnp.bfloat16)
    imag[...] = (
        (over_rows(sink[0], prop[1]) - over_rows(sink[1], prop[0])) * sign
    ).astype(jnp.bfloat16)
    half = sections // 2
    width = sections.bit_length() - 1
    rows = order // sections
    for q in range(sections):
        window = pl.ds(pl.multiple_of((section ^ q) * rows, rows), rows)
        slot = reversed_bits(q, width)
        (keep_real if slot < half else send_real)[slot % half] = real[window, :]
        (keep_imag if q < half else send_imag)[q % half] = imag[window, :]
    for copy in copies:
        copy.wait()


def hbm(value):
    return pltpu.with_memory_space_constraint(value, pltpu.HBM)


def products(live_rows, source_times, sink_vectors, propagators, sections):
    _, _, depth, order = sink_vectors.shape
    sources, columns = propagators.shape[0], propagators.shape[4]
    bf16 = jnp.bfloat16
    in_hbm, in_vmem = pl.BlockSpec(memory_space=pltpu.HBM), pl.BlockSpec(memory_space=pltpu.VMEM)
    half = pltpu.VMEM((sections // 2, order // sections, columns), bf16)
    held = pltpu.VMEM((2, depth, order), bf16)
    fetched = pltpu.VMEM((2, depth, columns), bf16)
    halves, sink, prop = [], None, None
    for source in range(sources):
        first, last = source == 0, source == sources - 1
        if first:
            operands = [hbm(live_rows), hbm(source_times), hbm(sink_vectors), hbm(propagators)]
            in_specs = [in_hbm] * 4
        else:
            operands = [hbm(source_times), sink, prop, hbm(propagators)]
            in_specs = [in_hbm, in_vmem, in_vmem, in_hbm]
        outs = [half] * 4 + [held] * first + [fetched] * (not last)
        scratch = [
            pltpu.VMEM((order, columns), bf16),
            pltpu.VMEM((order, columns), bf16),
            pltpu.SMEM(source_times.shape, jnp.int32),
            pltpu.SemaphoreType.DMA((6,)),
            pltpu.SemaphoreType.DMA((2,)),
        ]
        if first:
            scratch += [pltpu.SMEM(live_rows.shape, jnp.int32), held, fetched]
        results = pl.pallas_call(
            functools.partial(product_kernel, sections, source, sources),
            in_specs=in_specs,
            out_specs=[in_vmem] * len(outs),
            out_shape=outs,
            scratch_shapes=scratch,
            compiler_params=pltpu.CompilerParams(vmem_limit_bytes=24 << 20),
            cost_estimate=pl.CostEstimate(
                flops=8 * order * depth * columns,
                bytes_accessed=4 * depth * columns,
                transcendentals=0,
            ),
        )(*operands)
        halves.append(results[:4])
        if first:
            sink = results[4]
        prop = results[-1]
    return halves


def reduced(keep_real, send_real, keep_imag, send_imag, width):
    for step in range(width):
        got_real = exchanged(send_real, "sec", 1 << step)
        got_imag = exchanged(send_imag, "sec", 1 << (width - 1 - step))
        real = keep_real.astype(jnp.float32) + got_real.astype(jnp.float32)
        imag = keep_imag.astype(jnp.float32) + got_imag.astype(jnp.float32)
        real, imag = real.astype(jnp.bfloat16), imag.astype(jnp.bfloat16)
        half = real.shape[0] // 2
        if half:
            keep_real, send_real = real[:half], real[half:]
            keep_imag, send_imag = imag[:half], imag[half:]
    return jnp.concatenate((real, imag), 0)


def gathered(own, width):
    count = own.shape[0]
    whole = {0: own}
    places = [[((own, (s, 0)), (own, (s, 1)))] for s in range(count)]
    for q in range(1, 1 << width):
        high = 1 << (q.bit_length() - 1)
        low = q & -q
        if high == low:
            whole[q] = exchanged(own, "sec", high)
        for s in range(count):
            if high == low:
                places[s].append(((whole[q], (s, 0)), (whole[q], (s, 1))))
                continue
            (first, at_first), (second, at_second) = places[s][q ^ high][0], places[s][q ^ low][1]
            places[s].append(
                (
                    (exchanged(first[at_first], "sec", high), ()),
                    (exchanged(second[at_second], "sec", low), ()),
                )
            )
    return places


def sandwich_kernel(scale, lookup, source, kind, aliased, passed_on, *refs):
    left_real, left_imag = refs[0], refs[1]
    names = 1 + max(name for pair in lookup for name, _ in pair)
    blocks = refs[2 : 2 + names]
    rest = list(refs[2 + names + aliased :])
    out = rest.pop(0)
    real = [blocks[name][at if at else ...] for (name, at), _ in lookup]
    imag = [blocks[name][at if at else ...] for _, (name, at) in lookup]
    if passed_on:
        together = rest.pop(0)
        for q, pair in enumerate(zip(real, imag)):
            for part in range(2):
                together[q, part] = pair[part]
    tile, sems = rest
    right_real, right_imag = jnp.concatenate(real, 0), jnp.concatenate(imag, 0)
    one, two = left_real[...], left_imag[...]
    parity = lax.axis_index("ta") % 2
    stop = (2 * parity, 1, 2 - 2 * parity)[kind]
    shape = tile.shape[1:]
    copies = []
    for part in range(2):
        if part == 0:
            value = dot(one, right_real) - dot(two, right_imag)
        else:
            value = dot(one, right_imag) + dot(two, right_real)
        tile[part] = (value * scale).astype(jnp.bfloat16).reshape(shape)
        copies.append(
            pltpu.make_async_copy(tile.at[part], out.at[stop, :, source, part, 0], sems.at[part])
        )
        copies[-1].start()
    for copy in copies:
        copy.wait()


def sandwich(buffer, kind, source, left_real, left_imag, places, shape, passed_on=False):
    arrays, lookup = [], []
    for pair in places:
        entry = []
        for array, at in pair:
            known = [i for i, other in enumerate(arrays) if other is array]
            if not known:
                arrays.append(array)
                known = [len(arrays) - 1]
            entry.append((known[0], at))
        lookup.append(tuple(entry))
    order, columns = left_real.shape[1], shape[6]
    operands = [left_real, left_imag, *arrays]
    in_vmem, in_hbm = pl.BlockSpec(memory_space=pltpu.VMEM), pl.BlockSpec(memory_space=pltpu.HBM)
    in_specs = [in_vmem] * len(operands)
    aliases = {}
    if buffer is not None:
        aliases = {len(operands): 0}
        in_specs.append(in_hbm)
        operands.append(hbm(buffer))
    outs = [pltpu.HBM(shape, jnp.bfloat16)]
    if passed_on:
        outs.append(pltpu.VMEM((len(places), 2, shape[5], columns), jnp.bfloat16))
    return pl.pallas_call(
        functools.partial(
            sandwich_kernel, 0.5 * order ** (-0.5), tuple(lookup), source, kind,
            len(aliases), passed_on,
        ),
        in_specs=in_specs,
        out_specs=[in_hbm, in_vmem][: len(outs)],
        out_shape=outs,
        scratch_shapes=[
            pltpu.VMEM((2, shape[1]) + tuple(shape[5:]), jnp.bfloat16),
            pltpu.SemaphoreType.DMA((2,)),
        ],
        input_output_aliases=aliases,
        compiler_params=pltpu.CompilerParams(vmem_limit_bytes=12 << 20),
        cost_estimate=pl.CostEstimate(
            flops=8 * left_real.shape[0] * order * columns,
            bytes_accessed=4 * order * columns + 8 * left_real.size,
            transcendentals=0,
        ),
    )(*operands)


def body(sink_vectors, propagators, live_rows, source_times):
    sections = lax.axis_size("sec")
    width = sections.bit_length() - 1
    section = lax.axis_index("sec")
    first_core = lax.axis_index("ta") % 2 == 0
    sources = propagators.shape[0]
    order = sink_vectors.shape[3]
    rows = order // sections

    halves = products(live_rows, source_times, sink_vectors, propagators, sections)
    own = [reduced(*halves[s], width) for s in range(sources)]
    second = [shifted(own[s], 2) for s in range(sources)]
    mine, theirs = jnp.stack(own), jnp.stack(second)
    other = shifted(jnp.where(first_core, mine, theirs), 1)

    left = jnp.swapaxes(mine, 0, 1)
    left = jnp.concatenate(
        [
            lax.dynamic_slice_in_dim(left, (section ^ q) * rows, rows, axis=3)
            for q in range(sections)
        ],
        3,
    ).reshape(2, sources * rows, order)
    left_real, left_imag = left[0], left[1]

    shape = (STOPS, sources, sources, 2, 1, rows, order)
    result = None
    for s in range(sources):
        (places,) = gathered(second[s][None], width)
        result, together = sandwich(result, 1, s, left_real, left_imag, places, shape, True)
        together = exchanged(together, "ta", 1)
        places = [tuple((together, (q, part)) for part in range(2)) for q in range(sections)]
        (result,) = sandwich(result, 0, s, left_real, left_imag, places, shape)
    for s, places in enumerate(gathered(other, width)):
        (result,) = sandwich(result, 2, s, left_real, left_imag, places, shape)
    return result


def solution(mesh):
    return jax.shard_map(
        body,
        mesh=mesh,
        in_specs=(P(None, "ta", "sec", None), P(None, None, "ta", "sec", None), P(), P()),
        out_specs=P(None, None, None, None, "ta", "sec", None),
        check_vma=False,
    )
```

```python
import functools

import jax
import jax.numpy as jnp
from jax import lax
from jax.experimental import pallas as pl
from jax.experimental.pallas import tpu as pltpu
from jax.sharding import PartitionSpec as P

STOPS = 3
dot = functools.partial(jnp.dot, preferred_element_type=jnp.float32)


def shifted(value, steps):
    count = lax.axis_size("ta")
    pairs = [(source, (source + steps) % count) for source in range(count)]
    return lax.ppermute(value, "ta", pairs)


def exchanged(value, axis, bit):
    count = lax.axis_size(axis)
    return lax.ppermute(value, axis, [(source, source ^ bit) for source in range(count)])


def reversed_bits(value, width):
    return sum(((value >> place) & 1) << (width - 1 - place) for place in range(width))


def over_rows(left, right):
    return lax.dot_general(
        left, right, (((0,), (0,)), ((), ())), preferred_element_type=jnp.float32
    )


def product_kernel(sections, source, sources, *refs):
    refs = list(refs)
    first, last = source == 0, source == sources - 1
    if first:
        live_hbm, times_hbm, sink_hbm, prop_hbm = refs[:4]
        refs = refs[4:]
    else:
        times_hbm, sink, prop, prop_hbm = refs[:4]
        refs = refs[4:]
    keep_real, send_real, keep_imag, send_imag = refs[:4]
    refs = refs[4:]
    if first:
        sink = refs.pop(0)
    following = None if last else refs.pop(0)
    real, imag, times, sems, index_sems = refs[:5]
    refs = refs[5:]
    index_copies = [pltpu.make_async_copy(times_hbm, times, index_sems.at[0])]
    copies = []
    if first:
        live_rows, raw, prop = refs
        index_copies.append(pltpu.make_async_copy(live_hbm, live_rows, index_sems.at[1]))
        for part in range(2):
            copies.append(pltpu.make_async_copy(sink_hbm.at[part, 0], raw.at[part], sems.at[part]))
            copies.append(
                pltpu.make_async_copy(prop_hbm.at[0, part, 0], prop.at[part], sems.at[2 + part])
            )
    if not last:
        for part in range(2):
            copies.append(
                pltpu.make_async_copy(
                    prop_hbm.at[source + 1, part, 0], following.at[part], sems.at[4 + part]
                )
            )
    ahead = copies[-2:] if not last else []
    copies = copies[: len(copies) - len(ahead)]
    for copy in copies + index_copies:
        copy.start()
    section = lax.axis_index("sec")
    depth, order = sink.shape[1:]
    for copy in index_copies:
        copy.wait()
    sign = jnp.where(lax.axis_index("ta") < times[source], -1.0, 1.0).astype(jnp.float32)
    if first:
        live = lax.broadcasted_iota(jnp.int32, (depth, order), 0) < live_rows[section]
        for part in range(2):
            copies.pop(0).wait()
            sink[part] = jnp.where(live, raw[part], jnp.zeros((depth, order), jnp.bfloat16))
            copies.pop(0).wait()
            if part == 0:
                for copy in ahead:
                    copy.start()
                start = over_rows(sink[0], prop[0])
        real[...] = ((start + over_rows(sink[1], prop[1])) * sign).astype(jnp.bfloat16)
    else:
        for copy in ahead:
            copy.start()
        real[...] = (
            (over_rows(sink[0], prop[0]) + over_rows(sink[1], prop[1])) * sign
        ).astype(jnp.bfloat16)
    imag[...] = (
        (over_rows(sink[0], prop[1]) - over_rows(sink[1], prop[0])) * sign
    ).astype(jnp.bfloat16)
    half = sections // 2
    width = sections.bit_length() - 1
    rows = order // sections
    for q in range(sections):
        window = pl.ds(pl.multiple_of((section ^ q) * rows, rows), rows)
        slot = reversed_bits(q, width)
        (keep_real if slot < half else send_real)[slot % half] = real[window, :]
        (keep_imag if q < half else send_imag)[q % half] = imag[window, :]
    for copy in ahead:
        copy.wait()


def hbm(value):
    return pltpu.with_memory_space_constraint(value, pltpu.HBM)


def products(live_rows, source_times, sink_vectors, propagators, sections):
    _, _, depth, order = sink_vectors.shape
    sources, columns = propagators.shape[0], propagators.shape[4]
    bf16 = jnp.bfloat16
    in_hbm, in_vmem = pl.BlockSpec(memory_space=pltpu.HBM), pl.BlockSpec(memory_space=pltpu.VMEM)
    half = pltpu.VMEM((sections // 2, order // sections, columns), bf16)
    held = pltpu.VMEM((2, depth, order), bf16)
    fetched = pltpu.VMEM((2, depth, columns), bf16)
    halves, sink, prop = [], None, None
    for source in range(sources):
        first, last = source == 0, source == sources - 1
        if first:
            operands = [hbm(live_rows), hbm(source_times), hbm(sink_vectors), hbm(propagators)]
            in_specs = [in_hbm] * 4
        else:
            operands = [hbm(source_times), sink, prop, hbm(propagators)]
            in_specs = [in_hbm, in_vmem, in_vmem, in_hbm]
        outs = [half] * 4 + [held] * first + [fetched] * (not last)
        scratch = [
            pltpu.VMEM((order, columns), bf16),
            pltpu.VMEM((order, columns), bf16),
            pltpu.SMEM(source_times.shape, jnp.int32),
            pltpu.SemaphoreType.DMA((6,)),
            pltpu.SemaphoreType.DMA((2,)),
        ]
        if first:
            scratch += [pltpu.SMEM(live_rows.shape, jnp.int32), held, fetched]
        results = pl.pallas_call(
            functools.partial(product_kernel, sections, source, sources),
            in_specs=in_specs,
            out_specs=[in_vmem] * len(outs),
            out_shape=outs,
            scratch_shapes=scratch,
            compiler_params=pltpu.CompilerParams(vmem_limit_bytes=12 << 20),
            cost_estimate=pl.CostEstimate(
                flops=8 * order * depth * columns,
                bytes_accessed=4 * depth * columns,
                transcendentals=0,
            ),
        )(*operands)
        halves.append(results[:4])
        if first:
            sink = results[4]
        prop = results[-1]
    return halves


def added(kept, got):
    return (kept.astype(jnp.float32) + got.astype(jnp.float32)).astype(jnp.bfloat16)


def reduced(keep_real, send_real, keep_imag, send_imag, width):
    for step in range(width):
        got_real = exchanged(send_real, "sec", 1 << step)
        got_imag = exchanged(send_imag, "sec", 1 << (width - 1 - step))
        if step == width - 1:
            real = added(keep_real, got_real)
            imag = added(keep_imag, got_imag)
            return jnp.concatenate((real, imag), 0)
        real = added(keep_real, got_real)
        imag = added(keep_imag, got_imag)
        half = real.shape[0] // 2
        keep_real, send_real = real[:half], real[half:]
        keep_imag, send_imag = imag[:half], imag[half:]


def gathered(own, width):
    count = own.shape[0]
    whole = {0: own}
    places = [[((own, (s, 0)), (own, (s, 1)))] for s in range(count)]
    for q in range(1, 1 << width):
        high = 1 << (q.bit_length() - 1)
        low = q & -q
        if high == low:
            whole[q] = exchanged(own, "sec", high)
        for s in range(count):
            if high == low:
                places[s].append(((whole[q], (s, 0)), (whole[q], (s, 1))))
                continue
            (first, at_first), (second, at_second) = places[s][q ^ high][0], places[s][q ^ low][1]
            real = first[at_first]
            imag = second[at_second]
            places[s].append(
                ((exchanged(real, "sec", high), ()), (exchanged(imag, "sec", low), ()))
            )
    return places


def sandwich_kernel(scale, lookup, source, kind, aliased, passed_on, *refs):
    left_real, left_imag = refs[0], refs[1]
    names = 1 + max(name for pair in lookup for name, _ in pair)
    blocks = refs[2 : 2 + names]
    rest = list(refs[2 + names + aliased :])
    out = rest.pop(0)
    real = [blocks[name][at if at else ...] for (name, at), _ in lookup]
    imag = [blocks[name][at if at else ...] for _, (name, at) in lookup]
    if passed_on:
        together = rest.pop(0)
        for q, pair in enumerate(zip(real, imag)):
            for part in range(2):
                together[q, part] = pair[part]
    tile, sems = rest
    right_real, right_imag = jnp.concatenate(real, 0), jnp.concatenate(imag, 0)
    one, two = left_real[...], left_imag[...]
    parity = lax.axis_index("ta") % 2
    stop = (2 * parity, 1, 2 - 2 * parity)[kind]
    shape = tile.shape[1:]
    copies = []
    for part in range(2):
        if part == 0:
            value = dot(one, right_real) - dot(two, right_imag)
        else:
            value = dot(one, right_imag) + dot(two, right_real)
        tile[part] = (value * scale).astype(jnp.bfloat16).reshape(shape)
        copies.append(
            pltpu.make_async_copy(tile.at[part], out.at[stop, :, source, part, 0], sems.at[part])
        )
        copies[-1].start()
    for copy in copies:
        copy.wait()


def sandwich(buffer, kind, source, left_real, left_imag, places, shape, passed_on=False):
    arrays, lookup = [], []
    for pair in places:
        entry = []
        for array, at in pair:
            known = [i for i, other in enumerate(arrays) if other is array]
            if not known:
                arrays.append(array)
                known = [len(arrays) - 1]
            entry.append((known[0], at))
        lookup.append(tuple(entry))
    order, columns = left_real.shape[1], shape[6]
    operands = [left_real, left_imag, *arrays]
    in_vmem, in_hbm = pl.BlockSpec(memory_space=pltpu.VMEM), pl.BlockSpec(memory_space=pltpu.HBM)
    in_specs = [in_vmem] * len(operands)
    aliases = {}
    if buffer is not None:
        aliases = {len(operands): 0}
        in_specs.append(in_hbm)
        operands.append(hbm(buffer))
    outs = [pltpu.HBM(shape, jnp.bfloat16)]
    if passed_on:
        outs.append(pltpu.VMEM((len(places), 2, shape[5], columns), jnp.bfloat16))
    return pl.pallas_call(
        functools.partial(
            sandwich_kernel, 0.5 * order ** (-0.5), tuple(lookup), source, kind,
            len(aliases), passed_on,
        ),
        in_specs=in_specs,
        out_specs=[in_hbm, in_vmem][: len(outs)],
        out_shape=outs,
        scratch_shapes=[
            pltpu.VMEM((2, shape[1]) + tuple(shape[5:]), jnp.bfloat16),
            pltpu.SemaphoreType.DMA((2,)),
        ],
        input_output_aliases=aliases,
        compiler_params=pltpu.CompilerParams(vmem_limit_bytes=12 << 20),
        cost_estimate=pl.CostEstimate(
            flops=8 * left_real.shape[0] * order * columns,
            bytes_accessed=4 * order * columns + 8 * left_real.size,
            transcendentals=0,
        ),
    )(*operands)


def body(sink_vectors, propagators, live_rows, source_times):
    sections = lax.axis_size("sec")
    width = sections.bit_length() - 1
    sources = propagators.shape[0]
    order = sink_vectors.shape[3]
    rows = order // sections
    section = lax.axis_index("sec").astype(jnp.uint32)
    first_core = lax.axis_index("ta").astype(jnp.uint32) & 1 == 0
    offsets = [(section ^ q) * jnp.uint32(rows) for q in range(sections)]
    sink_vectors, first_core, offsets = lax.optimization_barrier(
        (sink_vectors, first_core, offsets)
    )

    halves = products(live_rows, source_times, sink_vectors, propagators, sections)
    own = [reduced(*halves[s], width) for s in range(sources)]
    second = [shifted(own[s], 2) for s in range(sources)]
    groups = ((0,), tuple(range(1, sources)))
    other = []
    for group in groups:
        chosen = jnp.stack([jnp.where(first_core, own[s], second[s]) for s in group])
        other.append(shifted(chosen, 1))

    left = jnp.stack(own, 1)
    zero = jnp.uint32(0)
    left = jnp.concatenate(
        [
            lax.dynamic_slice(left, (zero, zero, zero, offset), (2, sources, rows, rows))
            for offset in offsets
        ],
        3,
    ).reshape(2, sources * rows, order)
    left_real, left_imag = left[0], left[1]

    shape = (STOPS, sources, sources, 2, 1, rows, order)
    result = None
    swapped = {}

    def far(result, s):
        (places,) = gathered(second[s][None], width)
        result, together = sandwich(result, 1, s, left_real, left_imag, places, shape, True)
        swapped[s] = exchanged(together, "ta", 1)
        return result

    def near(result, s):
        places = [
            tuple((swapped[s], (q, part)) for part in range(2)) for q in range(sections)
        ]
        return sandwich(result, 0, s, left_real, left_imag, places, shape)[0]

    for s in range(sources):
        result = far(result, s)
        if 0 < s < sources - 1:
            result = near(result, s - 1)
            if s == sources - 2:
                result = near(result, s)
    result = near(result, sources - 1)
    for i, group in enumerate(groups):
        for s, places in zip(group, gathered(other[i], width)):
            (result,) = sandwich(result, 2, s, left_real, left_imag, places, shape)
    return result


def solution(mesh):
    return jax.shard_map(
        body,
        mesh=mesh,
        in_specs=(P(None, "ta", "sec", None), P(None, None, "ta", "sec", None), P(), P()),
        out_specs=P(None, None, None, None, "ta", "sec", None),
        check_vma=False,
    )
```

```python
import functools

import jax
import jax.numpy as jnp
from jax import lax
from jax.experimental import pallas as pl
from jax.experimental.pallas import tpu as pltpu
from jax.sharding import PartitionSpec as P

STOPS = 3
dot = functools.partial(jnp.dot, preferred_element_type=jnp.float32)


def shifted(value, steps, first=0, stride=1):
    count = lax.axis_size("ta")
    pairs = [(source, (source + steps) % count) for source in range(first, count, stride)]
    return lax.ppermute(value, "ta", pairs)


def swapped_cores(value):
    count = lax.axis_size("ta")
    return lax.ppermute(value, "ta", [(time, time ^ 1) for time in range(count)])


def exchanged(value, bit, first=0, stride=1):
    count, times = lax.axis_size("sec"), lax.axis_size("ta")
    flips = (bit, reversed_bits(bit, count.bit_length() - 1))
    pairs = [
        (section * times + time, (section ^ flips[time % 2]) * times + time)
        for section in range(count)
        for time in range(first, times, stride)
    ]
    return lax.ppermute(value, ("sec", "ta"), pairs)


def reversed_bits(value, width):
    return sum(((value >> place) & 1) << (width - 1 - place) for place in range(width))


def over_rows(left, right):
    return lax.dot_general(
        left, right, (((0,), (0,)), ((), ())), preferred_element_type=jnp.float32
    )


def product_kernel(sections, source, sources, *refs):
    refs = list(refs)
    first, last = source == 0, source == sources - 1
    if first:
        live_hbm, times_hbm, sink_hbm, prop_hbm = refs[:4]
        refs = refs[4:]
    else:
        times_hbm, sink, prop, prop_hbm = refs[:4]
        refs = refs[4:]
    keep, send = refs[:2]
    refs = refs[2:]
    if first:
        sink = refs.pop(0)
    following = None if last else refs.pop(0)
    real, imag, times, sems, index_sems = refs[:5]
    refs = refs[5:]
    index_copies = [pltpu.make_async_copy(times_hbm, times, index_sems.at[0])]
    copies = []
    if first:
        live_rows, raw, prop = refs
        index_copies.append(pltpu.make_async_copy(live_hbm, live_rows, index_sems.at[1]))
        for part in range(2):
            copies.append(pltpu.make_async_copy(sink_hbm.at[part, 0], raw.at[part], sems.at[part]))
            copies.append(
                pltpu.make_async_copy(prop_hbm.at[0, part, 0], prop.at[part], sems.at[2 + part])
            )
    if not last:
        for part in range(2):
            copies.append(
                pltpu.make_async_copy(
                    prop_hbm.at[source + 1, part, 0], following.at[part], sems.at[4 + part]
                )
            )
    ahead = copies[-2:] if not last else []
    copies = copies[: len(copies) - len(ahead)]
    for copy in copies + index_copies:
        copy.start()
    section = lax.axis_index("sec")
    depth, order = sink.shape[1:]
    for copy in index_copies:
        copy.wait()
    sign = jnp.where(lax.axis_index("ta") < times[source], -1.0, 1.0).astype(jnp.float32)
    if first:
        live = lax.broadcasted_iota(jnp.int32, (depth, order), 0) < live_rows[section]
        for part in range(2):
            copies.pop(0).wait()
            sink[part] = jnp.where(live, raw[part], jnp.zeros((depth, order), jnp.bfloat16))
            copies.pop(0).wait()
            if part == 0:
                for copy in ahead:
                    copy.start()
                start = over_rows(sink[0], prop[0])
        real[...] = ((start + over_rows(sink[1], prop[1])) * sign).astype(jnp.bfloat16)
    else:
        for copy in ahead:
            copy.start()
        real[...] = (
            (over_rows(sink[0], prop[0]) + over_rows(sink[1], prop[1])) * sign
        ).astype(jnp.bfloat16)
    imag[...] = (
        (over_rows(sink[0], prop[1]) - over_rows(sink[1], prop[0])) * sign
    ).astype(jnp.bfloat16)
    half = sections // 2
    width = sections.bit_length() - 1
    rows = order // sections
    for q in range(sections):
        slot = reversed_bits(q, width)
        flip = jnp.where(lax.axis_index("ta") % 2 == 0, q, slot)
        window = pl.ds(pl.multiple_of((section ^ flip) * rows, rows), rows)
        target = keep if slot < half else send
        target[slot % half, 0] = real[window, :]
        target[slot % half, 1] = imag[window, :]
    for copy in ahead:
        copy.wait()


def hbm(value):
    return pltpu.with_memory_space_constraint(value, pltpu.HBM)


def products(live_rows, source_times, sink_vectors, propagators, sections):
    _, _, depth, order = sink_vectors.shape
    sources, columns = propagators.shape[0], propagators.shape[4]
    bf16 = jnp.bfloat16
    in_hbm, in_vmem = pl.BlockSpec(memory_space=pltpu.HBM), pl.BlockSpec(memory_space=pltpu.VMEM)
    half = pltpu.VMEM((sections // 2, 2, order // sections, columns), bf16)
    held = pltpu.VMEM((2, depth, order), bf16)
    fetched = pltpu.VMEM((2, depth, columns), bf16)
    halves, sink, prop = [], None, None
    for source in range(sources):
        first, last = source == 0, source == sources - 1
        if first:
            operands = [hbm(live_rows), hbm(source_times), hbm(sink_vectors), hbm(propagators)]
            in_specs = [in_hbm] * 4
        else:
            operands = [hbm(source_times), sink, prop, hbm(propagators)]
            in_specs = [in_hbm, in_vmem, in_vmem, in_hbm]
        outs = [half] * 2 + [held] * first + [fetched] * (not last)
        scratch = [
            pltpu.VMEM((order, columns), bf16),
            pltpu.VMEM((order, columns), bf16),
            pltpu.SMEM(source_times.shape, jnp.int32),
            pltpu.SemaphoreType.DMA((6,)),
            pltpu.SemaphoreType.DMA((2,)),
        ]
        if first:
            scratch += [pltpu.SMEM(live_rows.shape, jnp.int32), held, fetched]
        results = pl.pallas_call(
            functools.partial(product_kernel, sections, source, sources),
            in_specs=in_specs,
            out_specs=[in_vmem] * len(outs),
            out_shape=outs,
            scratch_shapes=scratch,
            compiler_params=pltpu.CompilerParams(vmem_limit_bytes=12 << 20),
            cost_estimate=pl.CostEstimate(
                flops=8 * order * depth * columns,
                bytes_accessed=4 * depth * columns,
                transcendentals=0,
            ),
        )(*operands)
        halves.append(results[:2])
        if first:
            sink = results[2]
        prop = results[-1]
    return halves


def added(kept, got):
    return (kept.astype(jnp.float32) + got.astype(jnp.float32)).astype(jnp.bfloat16)


def reduced(keep, send, width):
    for step in range(width):
        got = exchanged(send, 1 << step)
        total = added(keep, got)
        half = total.shape[0] // 2
        keep, send = total[:half], total[half:]
    return total[0]


def gathered(own, width, **among):
    whole = [own]
    for q in range(1, 1 << width):
        high = 1 << (q.bit_length() - 1)
        whole.append(exchanged(whole[q ^ high], high, **among))
    return [
        [tuple((piece, (s, part)) for part in range(2)) for piece in whole]
        for s in range(own.shape[0])
    ]


def sandwich_kernel(scale, jobs, names, aliased, *refs):
    left_real, left_imag = refs[0], refs[1]
    blocks = refs[2 : 2 + names]
    rest = list(refs[2 + names + aliased :])
    out = rest.pop(0)
    tile, sems = rest
    parity = lax.axis_index("ta") % 2
    shape = tile.shape[2:]

    def run(job, lookup):
        real = [blocks[name][at] for (name, at), _ in lookup]
        imag = [blocks[name][at] for _, (name, at) in lookup]
        right_real, right_imag = jnp.concatenate(real, 0), jnp.concatenate(imag, 0)
        one, two = left_real[...], left_imag[...]
        for part in range(2):
            if part == 0:
                value = dot(one, right_real) - dot(two, right_imag)
            else:
                value = dot(one, right_imag) + dot(two, right_real)
            tile[job, part] = (value * scale).astype(jnp.bfloat16).reshape(shape)
            copies[job][part].start()

    copies = []
    for job, (kind, source, _) in enumerate(jobs):
        stop = (2 * parity, 1, 2 - 2 * parity)[kind]
        copies.append(
            [
                pltpu.make_async_copy(
                    tile.at[job, part], out.at[stop, :, source, part, 0], sems.at[job, part]
                )
                for part in range(2)
            ]
        )
    for job, (_, _, lookups) in enumerate(jobs):
        if len(lookups) == 1:
            run(job, lookups[0])
        else:
            for which in range(2):
                pl.when(parity == which)(functools.partial(run, job, lookups[which]))
    for pair in copies:
        for copy in pair:
            copy.wait()


def sandwich(buffer, jobs, left_real, left_imag, shape):
    arrays, described = [], []
    for kind, source, choices in jobs:
        lookups = []
        for places in choices:
            lookup = []
            for pair in places:
                entry = []
                for array, at in pair:
                    known = [i for i, other in enumerate(arrays) if other is array]
                    if not known:
                        arrays.append(array)
                        known = [len(arrays) - 1]
                    entry.append((known[0], at))
                lookup.append(tuple(entry))
            lookups.append(tuple(lookup))
        described.append((kind, source, tuple(lookups)))
    order, columns = left_real.shape[1], shape[6]
    operands = [left_real, left_imag, *arrays]
    in_vmem, in_hbm = pl.BlockSpec(memory_space=pltpu.VMEM), pl.BlockSpec(memory_space=pltpu.HBM)
    in_specs = [in_vmem] * len(operands)
    aliases = {}
    if buffer is not None:
        aliases = {len(operands): 0}
        in_specs.append(in_hbm)
        operands.append(hbm(buffer))
    return pl.pallas_call(
        functools.partial(
            sandwich_kernel, 0.5 * order ** (-0.5), tuple(described), len(arrays), len(aliases)
        ),
        in_specs=in_specs,
        out_specs=in_hbm,
        out_shape=pltpu.HBM(shape, jnp.bfloat16),
        scratch_shapes=[
            pltpu.VMEM((len(jobs), 2, shape[1]) + tuple(shape[5:]), jnp.bfloat16),
            pltpu.SemaphoreType.DMA((len(jobs), 2)),
        ],
        input_output_aliases=aliases,
        compiler_params=pltpu.CompilerParams(vmem_limit_bytes=14 << 20),
        cost_estimate=pl.CostEstimate(
            flops=8 * len(jobs) * left_real.shape[0] * order * columns,
            bytes_accessed=4 * len(jobs) * left_real.size,
            transcendentals=0,
        ),
    )(*operands)


def body(sink_vectors, propagators, live_rows, source_times):
    sections = lax.axis_size("sec")
    width = sections.bit_length() - 1
    sources = propagators.shape[0]
    order = sink_vectors.shape[3]
    rows = order // sections
    section = lax.axis_index("sec").astype(jnp.uint32)
    first_core = lax.axis_index("ta").astype(jnp.uint32) & 1 == 0
    offsets = [
        (section ^ jnp.where(first_core, jnp.uint32(q), jnp.uint32(reversed_bits(q, width))))
        * jnp.uint32(rows)
        for q in range(sections)
    ]
    sink_vectors, first_core, offsets = lax.optimization_barrier(
        (sink_vectors, first_core, offsets)
    )

    halves = products(live_rows, source_times, sink_vectors, propagators, sections)
    own = [reduced(*halves[s], width) for s in range(sources)]
    second = [shifted(own[s], 2) for s in range(sources)]
    forwarded = tuple(range(sources - 1))
    groups = (forwarded, (sources - 1,))
    last = {}
    for group in groups:
        chosen = jnp.stack(
            [own[s] if s in forwarded else jnp.where(first_core, own[s], second[s]) for s in group]
        )
        if group[0] in forwarded:
            chosen = shifted(chosen, 1, stride=2)
            places = gathered(chosen, width, first=1, stride=2)
        else:
            chosen = shifted(chosen, 1)
            places = gathered(chosen, width)
        last.update(zip(group, places))

    left = jnp.stack(own, 1)
    zero = jnp.uint32(0)
    left = jnp.concatenate(
        [
            lax.dynamic_slice(left, (zero, zero, zero, offset), (2, sources, rows, rows))
            for offset in offsets
        ],
        3,
    ).reshape(2, sources * rows, order)
    left_real, left_imag = left[0], left[1]

    shape = (STOPS, sources, sources, 2, 1, rows, order)
    far, swapped, ahead = {}, {}, {}
    for s in range(sources):
        (far[s],) = gathered(second[s][None], width)
        together = jnp.concatenate([pair[0][0] for pair in far[s]], 0)
        swapped[s] = swapped_cores(together)
        if s in forwarded:
            ahead[s] = shifted(together, 1, first=1, stride=2)

    def whole(value):
        return [
            tuple((value, (reversed_bits(q, width), part)) for part in range(2))
            for q in range(sections)
        ]

    def step(result, jobs):
        listed = []
        for kind, s in jobs:
            if kind == 1:
                choices = (far[s],)
            elif kind == 0:
                choices = (whole(swapped[s]),)
            else:
                choices = (whole(ahead[s]), last[s]) if s in forwarded else (last[s],)
            listed.append((kind, s, choices))
        return sandwich(result, listed, left_real, left_imag, shape)

    result = None
    tail = sources - 1
    calls = [[(1, s), (0, s)] for s in range(tail)] + [[(1, tail)], [(0, tail), (2, 0)]]
    calls += [[(2, s)] for s in range(tail, 0, -1)]
    for jobs in calls:
        result = step(result, jobs)
    return result


def solution(mesh):
    return jax.shard_map(
        body,
        mesh=mesh,
        in_specs=(P(None, "ta", "sec", None), P(None, None, "ta", "sec", None), P(), P()),
        out_specs=P(None, None, None, None, "ta", "sec", None),
        check_vma=False,
    )
```

```python
import functools

import jax
import jax.numpy as jnp
from jax import lax
from jax.experimental import pallas as pl
from jax.experimental.pallas import tpu as pltpu
from jax.sharding import PartitionSpec as P

STOPS = 3
dot = functools.partial(jnp.dot, preferred_element_type=jnp.float32)


def shifted(value, steps, first=0, stride=1):
    count = lax.axis_size("ta")
    pairs = [(source, (source + steps) % count) for source in range(first, count, stride)]
    return lax.ppermute(value, "ta", pairs)


def swapped_cores(value):
    count = lax.axis_size("ta")
    return lax.ppermute(value, "ta", [(time, time ^ 1) for time in range(count)])


def exchanged(value, bit, first=0, stride=1):
    count, times = lax.axis_size("sec"), lax.axis_size("ta")
    flips = (bit, reversed_bits(bit, count.bit_length() - 1))
    pairs = [
        (section * times + time, (section ^ flips[time % 2]) * times + time)
        for section in range(count)
        for time in range(first, times, stride)
    ]
    return lax.ppermute(value, ("sec", "ta"), pairs)


def reversed_bits(value, width):
    return sum(((value >> place) & 1) << (width - 1 - place) for place in range(width))


def over_rows(left, right):
    return lax.dot_general(
        left, right, (((0,), (0,)), ((), ())), preferred_element_type=jnp.float32
    )


def product_kernel(sections, source, sources, *refs):
    refs = list(refs)
    first, last = source == 0, source == sources - 1
    if first:
        live_hbm, times_hbm, sink_hbm, prop_hbm = refs[:4]
        refs = refs[4:]
    else:
        times_hbm, sink, prop, prop_hbm = refs[:4]
        refs = refs[4:]
    keep, send = refs[:2]
    refs = refs[2:]
    if first:
        sink = refs.pop(0)
    following = None if last else refs.pop(0)
    real, imag, times, sems, index_sems = refs[:5]
    refs = refs[5:]
    index_copies = [pltpu.make_async_copy(times_hbm, times, index_sems.at[0])]
    copies = []
    if first:
        live_rows, raw, prop = refs
        index_copies.append(pltpu.make_async_copy(live_hbm, live_rows, index_sems.at[1]))
        for part in range(2):
            copies.append(pltpu.make_async_copy(sink_hbm.at[part, 0], raw.at[part], sems.at[part]))
            copies.append(
                pltpu.make_async_copy(prop_hbm.at[0, part, 0], prop.at[part], sems.at[2 + part])
            )
    if not last:
        for part in range(2):
            copies.append(
                pltpu.make_async_copy(
                    prop_hbm.at[source + 1, part, 0], following.at[part], sems.at[4 + part]
                )
            )
    ahead = copies[-2:] if not last else []
    copies = copies[: len(copies) - len(ahead)]
    for copy in copies + index_copies:
        copy.start()
    section = lax.axis_index("sec")
    depth, order = sink.shape[1:]
    for copy in index_copies:
        copy.wait()
    sign = jnp.where(lax.axis_index("ta") < times[source], -1.0, 1.0).astype(jnp.float32)
    if first:
        live = lax.broadcasted_iota(jnp.int32, (depth, order), 0) < live_rows[section]
        for part in range(2):
            copies.pop(0).wait()
            sink[part] = jnp.where(live, raw[part], jnp.zeros((depth, order), jnp.bfloat16))
            copies.pop(0).wait()
            if part == 0:
                for copy in ahead:
                    copy.start()
                start = over_rows(sink[0], prop[0])
        real[...] = ((start + over_rows(sink[1], prop[1])) * sign).astype(jnp.bfloat16)
    else:
        for copy in ahead:
            copy.start()
        real[...] = (
            (over_rows(sink[0], prop[0]) + over_rows(sink[1], prop[1])) * sign
        ).astype(jnp.bfloat16)
    imag[...] = (
        (over_rows(sink[0], prop[1]) - over_rows(sink[1], prop[0])) * sign
    ).astype(jnp.bfloat16)
    half = sections // 2
    width = sections.bit_length() - 1
    rows = order // sections
    for q in range(sections):
        slot = reversed_bits(q, width)
        flip = jnp.where(lax.axis_index("ta") % 2 == 0, q, slot)
        window = pl.ds(pl.multiple_of((section ^ flip) * rows, rows), rows)
        target = keep if slot < half else send
        target[slot % half, 0] = real[window, :]
        target[slot % half, 1] = imag[window, :]
    for copy in ahead:
        copy.wait()


def hbm(value):
    return pltpu.with_memory_space_constraint(value, pltpu.HBM)


def products(live_rows, source_times, sink_vectors, propagators, sections):
    _, _, depth, order = sink_vectors.shape
    sources, columns = propagators.shape[0], propagators.shape[4]
    bf16 = jnp.bfloat16
    in_hbm, in_vmem = pl.BlockSpec(memory_space=pltpu.HBM), pl.BlockSpec(memory_space=pltpu.VMEM)
    half = pltpu.VMEM((sections // 2, 2, order // sections, columns), bf16)
    held = pltpu.VMEM((2, depth, order), bf16)
    fetched = pltpu.VMEM((2, depth, columns), bf16)
    halves, sink, prop = [], None, None
    for source in range(sources):
        first, last = source == 0, source == sources - 1
        if first:
            operands = [hbm(live_rows), hbm(source_times), hbm(sink_vectors), hbm(propagators)]
            in_specs = [in_hbm] * 4
        else:
            operands = [hbm(source_times), sink, prop, hbm(propagators)]
            in_specs = [in_hbm, in_vmem, in_vmem, in_hbm]
        outs = [half] * 2 + [held] * first + [fetched] * (not last)
        scratch = [
            pltpu.VMEM((order, columns), bf16),
            pltpu.VMEM((order, columns), bf16),
            pltpu.SMEM(source_times.shape, jnp.int32),
            pltpu.SemaphoreType.DMA((6,)),
            pltpu.SemaphoreType.DMA((2,)),
        ]
        if first:
            scratch += [pltpu.SMEM(live_rows.shape, jnp.int32), held, fetched]
        results = pl.pallas_call(
            functools.partial(product_kernel, sections, source, sources),
            in_specs=in_specs,
            out_specs=[in_vmem] * len(outs),
            out_shape=outs,
            scratch_shapes=scratch,
            compiler_params=pltpu.CompilerParams(vmem_limit_bytes=12 << 20),
            cost_estimate=pl.CostEstimate(
                flops=8 * order * depth * columns,
                bytes_accessed=4 * depth * columns,
                transcendentals=0,
            ),
        )(*operands)
        halves.append(results[:2])
        if first:
            sink = results[2]
        prop = results[-1]
    return halves


def added(kept, got):
    return (kept.astype(jnp.float32) + got.astype(jnp.float32)).astype(jnp.bfloat16)


def reduced(keep, send, width):
    for step in range(width):
        got = exchanged(send, 1 << step)
        total = added(keep, got)
        half = total.shape[0] // 2
        keep, send = total[:half], total[half:]
    return total[0]


def gathered(own, width, **among):
    whole = [own]
    for q in range(1, 1 << width):
        high = 1 << (q.bit_length() - 1)
        whole.append(exchanged(whole[q ^ high], high, **among))
    return [
        [tuple((piece, (s, part)) for part in range(2)) for piece in whole]
        for s in range(own.shape[0])
    ]


def sandwich_kernel(scale, jobs, names, aliased, *refs):
    left_real, left_imag = refs[0], refs[1]
    blocks = refs[2 : 2 + names]
    rest = list(refs[2 + names + aliased :])
    out = rest.pop(0)
    tile, sems = rest
    parity = lax.axis_index("ta") % 2
    shape = tile.shape[2:]

    def run(job, lookup):
        real = [blocks[name][at] for (name, at), _ in lookup]
        imag = [blocks[name][at] for _, (name, at) in lookup]
        right_real, right_imag = jnp.concatenate(real, 0), jnp.concatenate(imag, 0)
        one, two = left_real[...], left_imag[...]
        for part in range(2):
            if part == 0:
                value = dot(one, right_real) - dot(two, right_imag)
            else:
                value = dot(one, right_imag) + dot(two, right_real)
            tile[job, part] = (value * scale).astype(jnp.bfloat16).reshape(shape)
            copies[job][part].start()

    copies = []
    for job, (kind, source, _) in enumerate(jobs):
        stop = (2 * parity, 1, 2 - 2 * parity)[kind]
        copies.append(
            [
                pltpu.make_async_copy(
                    tile.at[job, part], out.at[stop, :, source, part, 0], sems.at[job, part]
                )
                for part in range(2)
            ]
        )
    for job, (_, _, lookups) in enumerate(jobs):
        if len(lookups) == 1:
            run(job, lookups[0])
        else:
            for which in range(2):
                pl.when(parity == which)(functools.partial(run, job, lookups[which]))
    for pair in copies:
        for copy in pair:
            copy.wait()


def sandwich(buffer, jobs, left_real, left_imag, shape):
    arrays, described = [], []
    for kind, source, choices in jobs:
        lookups = []
        for places in choices:
            lookup = []
            for pair in places:
                entry = []
                for array, at in pair:
                    known = [i for i, other in enumerate(arrays) if other is array]
                    if not known:
                        arrays.append(array)
                        known = [len(arrays) - 1]
                    entry.append((known[0], at))
                lookup.append(tuple(entry))
            lookups.append(tuple(lookup))
        described.append((kind, source, tuple(lookups)))
    order, columns = left_real.shape[1], shape[6]
    operands = [left_real, left_imag, *arrays]
    in_vmem, in_hbm = pl.BlockSpec(memory_space=pltpu.VMEM), pl.BlockSpec(memory_space=pltpu.HBM)
    in_specs = [in_vmem] * len(operands)
    aliases = {}
    if buffer is not None:
        aliases = {len(operands): 0}
        in_specs.append(in_hbm)
        operands.append(hbm(buffer))
    return pl.pallas_call(
        functools.partial(
            sandwich_kernel, 0.5 * order ** (-0.5), tuple(described), len(arrays), len(aliases)
        ),
        in_specs=in_specs,
        out_specs=in_hbm,
        out_shape=pltpu.HBM(shape, jnp.bfloat16),
        scratch_shapes=[
            pltpu.VMEM((len(jobs), 2, shape[1]) + tuple(shape[5:]), jnp.bfloat16),
            pltpu.SemaphoreType.DMA((len(jobs), 2)),
        ],
        input_output_aliases=aliases,
        compiler_params=pltpu.CompilerParams(vmem_limit_bytes=14 << 20),
        cost_estimate=pl.CostEstimate(
            flops=8 * len(jobs) * left_real.shape[0] * order * columns,
            bytes_accessed=4 * len(jobs) * left_real.size,
            transcendentals=0,
        ),
    )(*operands)


def body(sink_vectors, propagators, live_rows, source_times):
    sections = lax.axis_size("sec")
    width = sections.bit_length() - 1
    sources = propagators.shape[0]
    order = sink_vectors.shape[3]
    rows = order // sections
    section = lax.axis_index("sec").astype(jnp.uint32)
    first_core = lax.axis_index("ta").astype(jnp.uint32) & 1 == 0
    offsets = [
        (section ^ jnp.where(first_core, jnp.uint32(q), jnp.uint32(reversed_bits(q, width))))
        * jnp.uint32(rows)
        for q in range(sections)
    ]
    sink_vectors, first_core, offsets = lax.optimization_barrier(
        (sink_vectors, first_core, offsets)
    )

    halves = products(live_rows, source_times, sink_vectors, propagators, sections)
    own = [reduced(*halves[s], width) for s in range(sources)]
    second = [shifted(own[s], 2) for s in range(sources)]
    forwarded = (0,)
    groups = (forwarded, tuple(range(1, sources)))
    last = {}
    for group in groups:
        chosen = jnp.stack(
            [own[s] if s in forwarded else jnp.where(first_core, own[s], second[s]) for s in group]
        )
        if group[0] in forwarded:
            chosen = shifted(chosen, 1, stride=2)
            places = gathered(chosen, width, first=1, stride=2)
        else:
            chosen = shifted(chosen, 1)
            places = gathered(chosen, width)
        last.update(zip(group, places))

    left = jnp.stack(own, 1)
    zero = jnp.uint32(0)
    left = jnp.concatenate(
        [
            lax.dynamic_slice(left, (zero, zero, zero, offset), (2, sources, rows, rows))
            for offset in offsets
        ],
        3,
    ).reshape(2, sources * rows, order)
    left_real, left_imag = left[0], left[1]

    shape = (STOPS, sources, sources, 2, 1, rows, order)
    far, swapped, ahead = {}, {}, {}
    for s in range(sources):
        (far[s],) = gathered(second[s][None], width)
        together = jnp.concatenate([pair[0][0] for pair in far[s]], 0)
        swapped[s] = swapped_cores(together)
        if s in forwarded:
            ahead[s] = shifted(together, 1, first=1, stride=2)

    def whole(value):
        return [
            tuple((value, (reversed_bits(q, width), part)) for part in range(2))
            for q in range(sections)
        ]

    def step(result, jobs):
        listed = []
        for kind, s in jobs:
            if kind == 1:
                choices = (far[s],)
            elif kind == 0:
                choices = (whole(swapped[s]),)
            else:
                choices = (whole(ahead[s]), last[s]) if s in forwarded else (last[s],)
            listed.append((kind, s, choices))
        return sandwich(result, listed, left_real, left_imag, shape)

    result = None
    tail = sources - 1
    middle = [(kind, s) for s in range(1, tail) for kind in (1, 0)]
    calls = [[(1, 0), (0, 0)], middle + [(1, tail)], [(0, tail), (2, 0)]]
    calls += [[(2, s) for s in range(1, sources)]]
    for jobs in calls:
        result = step(result, jobs)
    return result


def solution(mesh):
    return jax.shard_map(
        body,
        mesh=mesh,
        in_specs=(P(None, "ta", "sec", None), P(None, None, "ta", "sec", None), P(), P()),
        out_specs=P(None, None, None, None, "ta", "sec", None),
        check_vma=False,
    )
```
